32 devices in a mesh: frame: 16 (over z, y, x), head: 2 (over core).
Axes of the slice: x: 2, y: 2, z: 4, core: 2. Of those that a mesh axis runs over, the one named last changes fastest.
Arguments:
- residual: bfloat16 [2048, 5120], P('frame', 'head'), may hold values from -48 to 48
- query_proj: bfloat16 [2048, 3072], P('frame', 'head'), may hold values from -200 to 200
- key_proj: bfloat16 [2048, 3072], P('frame', 'head'), may hold values from -200 to 200
- value_proj: bfloat16 [2048, 3072], P('frame', 'head'), may hold values from -6 to 6
- q_gain: float32 [3072], P('head'), may hold values from 1 to 3
- k_gain: float32 [3072], P('head'), may hold values from 1 to 3
- time_embed: float32 [5120], P(('frame', 'head')), may hold values from -6 to 6
- time_proj: bfloat16 [5120, 3, 5120], P(('frame', 'head')), may hold values from -0.15625 to 0.15625
- mod_table: float32 [3, 5120], P(None, 'head'), may hold values from -3 to 3
- out_weight: bfloat16 [3072, 5120], P('head'), may hold values from -0.109375 to 0.109375
Outputs:
- hidden_out: bfloat16 [2048, 5120], P('frame', 'head')
- mlp_input: bfloat16 [2048, 5120], P('frame', 'head')
The draws below stay inside these ranges and needn't reach their ends.
All inputs are finite; a program needn't handle non-finite values.
Results may differ from the reference program's by a relative error of at most 0.0071.
Values may be sent and summed in bfloat16 or wider, within the bound.
A program may use at most 128 MiB of HBM per device.

```python
import math
import jax
import jax.numpy as jnp
from jax import lax

D = 5120
HEADS = 24
HD = 128
TOK_DEV = 128
HQ = 3072
TOKENS = 2048


def draw_residual(key, part):
    key_base, key_rows, key_cols = jax.random.split(key, 3)
    base = jnp.clip(jax.random.normal(key_base, (TOKENS, D)), -4.0, 4.0)
    rows = jnp.exp(jax.random.uniform(key_rows, (TOKENS, 1), minval=math.log(0.25), maxval=math.log(2.5)))
    trend = math.log(3.0) * jnp.arange(D, dtype=jnp.float32) / D
    cols = jnp.exp(trend + jax.random.uniform(key_cols, (D,), minval=-0.35, maxval=0.35))
    return (base * rows * cols).astype(jnp.bfloat16)


def random_field(key_base, key_rows, key_cols):
    base = jnp.clip(jax.random.normal(key_base, (TOKENS, HQ)), -4.0, 4.0)
    rows = jnp.exp(jax.random.uniform(key_rows, (TOKENS, 1), minval=0.0, maxval=math.log(10.0)))
    trend = 0.5 * math.log(3.0) * jnp.arange(HQ, dtype=jnp.float32) / HQ
    cols = jnp.exp(trend + jax.random.uniform(key_cols, (HQ,), minval=-1.0, maxval=1.0))
    return base * rows * cols


def paired_fields(key):
    seeds = jax.random.split(key, 6)
    queries = random_field(seeds[0], seeds[1], seeds[2])
    keys_field = random_field(seeds[3], seeds[4], seeds[5])
    return (queries, keys_field)


def draw_query_proj(key, part):
    return paired_fields(key)[0].astype(jnp.bfloat16)


def draw_key_proj(key, part):
    return paired_fields(key)[1].astype(jnp.bfloat16)


def strengthened(entries, rng, source, target, shards_of, factor):
    owner, partner = [(jnp.arange(entries.shape[position]) // (entries.shape[position] // shards_of)).reshape([-1 if axis == position else 1 for axis in range(entries.ndim)]) for position in (source, target)]
    chosen = jax.random.permutation(rng, shards_of)[partner]
    strong = (owner == chosen) | (owner == (partner + shards_of // 2) % shards_of)
    return jnp.where(strong, factor * entries, entries)


def steps_of(rng, shape, cuts, least, largest):
    def one(dim, blocks):
        draws = jax.random.uniform(jax.random.fold_in(jax.random.fold_in(rng, 6), dim), (blocks,), jnp.float32, least / len(cuts), largest / len(cuts))
        return jnp.repeat(jnp.exp(draws), shape[dim] // blocks).reshape((-1,) + (1,) * (len(shape) - dim - 1))

    loudness = one(*cuts[0])
    for cut in cuts[1:]:
        loudness = loudness * one(*cut)
    return loudness


def scatter_about(stream_key, dims, scale, reach, cuts=(), kind=jnp.bfloat16):
    array = jax.random.normal(stream_key, dims, jnp.float32) * scale
    if len(cuts) > 0:
        array = steps_of(stream_key, dims, cuts, -0.22, 0.18) * array
    return jnp.clip(array, min=-reach, max=reach).astype(kind)


def gaussian_with(stream_key, extent, deviation, reach, shards, heavy, held_as=jnp.bfloat16):
    entries = deviation * jax.random.normal(stream_key, extent, jnp.float32)
    if shards:
        entries = entries * steps_of(stream_key, extent, shards, -0.22, 0.18)
    return jnp.clip(strengthened(entries, jax.random.fold_in(stream_key, 3), *heavy), -reach, reach).astype(held_as)


def setup_inputs(seed: int = 0) -> dict:
    keys = jax.random.split(jax.random.key(seed), 11)
    return {
        "residual": draw_residual(jax.random.fold_in(keys[10], 71), 0),
        "query_proj": draw_query_proj(jax.random.fold_in(keys[10], 71), 0),
        "key_proj": draw_key_proj(jax.random.fold_in(keys[10], 71), 0),
        "value_proj": scatter_about(keys[3], (TOKENS, HQ), 1.0, 6.0, ((0, 16), (1, 2))),
        "q_gain": jnp.clip(jnp.exp(math.log(3.0) - 1.0986123 * jax.random.uniform(keys[4], (HQ,), jnp.float32) ** steps_of(keys[4], (HQ,), ((0, 2),), -0.2, 0.2)), 1.0, 3.0),
        "k_gain": jnp.clip(jnp.exp(math.log(3.0) - 1.0986123 * jax.random.uniform(keys[5], (HQ,), jnp.float32) ** steps_of(keys[5], (HQ,), ((0, 2),), -0.2, 0.2)), 1.0, 3.0),
        "time_embed": scatter_about(keys[6], (D,), 1.5, 6.0, ((0, 32),), jnp.float32),
        "time_proj": gaussian_with(keys[7], (D, 3, D), D ** -0.5, 0.15625, ((0, 32),), (0, 2, 32, 2.75)),
        "mod_table": scatter_about(keys[8], (3, D), 0.5, 3.0, ((1, 2),), jnp.float32),
        "out_weight": scatter_about(keys[9], (HQ, D), HQ ** -0.5, 0.109375, ((0, 2),)),
    }


def reference(residual, query_proj, key_proj, value_proj, q_gain, k_gain, time_embed, time_proj, mod_table, out_weight):
    emb = jax.nn.silu(time_embed)
    modulation = mod_table + jnp.einsum('r,rcd->cd', emb, time_proj.astype(jnp.float32), precision=lax.Precision.HIGHEST)
    gate = modulation[0]
    shift = modulation[1]
    scale = modulation[2]
    query_wide = query_proj.astype(jnp.float32)
    key_wide = key_proj.astype(jnp.float32)
    query_rms = lax.rsqrt(lax.optimization_barrier(jnp.sum(query_wide * query_wide, axis=1)) / (HEADS * HD) + 1e-06)
    key_rms = lax.rsqrt(lax.optimization_barrier(jnp.sum(key_wide * key_wide, axis=1)) / (HEADS * HD) + 1e-06)
    query_normed = (query_wide * query_rms[:, None] * q_gain).astype(jnp.bfloat16)
    key_normed = (key_wide * key_rms[:, None] * k_gain).astype(jnp.bfloat16)
    inv_root = 1.0 / math.sqrt(HD)
    q_heads = query_normed.reshape(TOKENS, HEADS, HD).transpose(1, 0, 2)
    k_heads = key_normed.reshape(TOKENS, HEADS, HD).transpose(1, 0, 2)
    v_heads = value_proj.reshape(TOKENS, HEADS, HD).transpose(1, 0, 2)

    def head_attend(packed):
        q_head, k_head, v_head = packed
        values = v_head.astype(jnp.float32)

        def block(q_block):
            scores = jnp.dot(q_block, k_head.T, preferred_element_type=jnp.float32) * inv_root
            top = lax.optimization_barrier(jnp.max(scores, axis=1, keepdims=True))
            weights = jnp.exp(scores - top)
            total = lax.optimization_barrier(jnp.sum(weights, axis=1, keepdims=True))
            return jnp.dot(weights, values, precision=lax.Precision.HIGHEST) / total
        blocks = lax.map(block, q_head.reshape(TOKENS // TOK_DEV, TOK_DEV, HD))
        return blocks.reshape(TOKENS, HD)
    attn_heads = lax.map(head_attend, (q_heads, k_heads, v_heads))
    attn = attn_heads.transpose(1, 0, 2).reshape(TOKENS, HEADS * HD).astype(jnp.bfloat16)
    proj = jnp.dot(attn, out_weight, preferred_element_type=jnp.float32)
    hidden_out = (residual.astype(jnp.float32) + gate * proj).astype(jnp.bfloat16)
    hidden32 = lax.optimization_barrier(hidden_out).astype(jnp.float32)
    mean = lax.optimization_barrier(jnp.sum(hidden32, axis=1, keepdims=True)) / D
    var = lax.optimization_barrier(jnp.sum(hidden32 * hidden32, axis=1, keepdims=True)) / D - mean * mean
    mlp_input = ((hidden32 - mean) * lax.rsqrt(var + 1e-06) * (1.0 + scale) + shift).astype(jnp.bfloat16)
    return (hidden_out, mlp_input)
```

```python
import math

import jax
import jax.numpy as jnp
from jax import lax
from jax.experimental import pallas as pl
from jax.experimental.pallas import tpu as pltpu
from jax.sharding import PartitionSpec as P

D = 5120
HEADS = 24
HD = 128


MESH = pl.DeviceIdType.MESH
PLANE = 4
LINE = 4
ORDER = ((0, 0), (0, 1), (1, 0), (3, 0), (2, 0), (1, 1), (3, 1), (2, 1))


def remote(src, dst, send, recv, device):
    return pltpu.make_async_remote_copy(
        src_ref=src, dst_ref=dst, send_sem=send, recv_sem=recv, device_id=device, device_id_type=MESH
    )


def attend_kernel(
    q_ref, k_ref, v_ref, part_ref, attn_ref, mod_ref,
    kbuf, vbuf, qbuf, obuf, arecv, mpart, macc, mline, mx, my,
    own_sem, zs, zr, xs, xr, ys, yr, dxs, dxr, dys, dyr, os, orr, ms, mr,
):
    frames = LINE * PLANE
    f = lax.axis_index("frame")
    hd = lax.axis_index("head")
    z = lax.div(f, PLANE)
    x = lax.rem(f, 2)
    y = lax.rem(lax.div(f, 2), 2)
    step_x = 1 - 2 * x
    step_y = 2 - 4 * y
    to_x = {"frame": f + step_x}
    to_y = {"frame": f + step_y}
    to_pair = {"head": 1 - hd}
    rows = q_ref.shape[0]
    half = rows // 2
    width = q_ref.shape[1] // LINE

    def later(d):
        return lax.rem(f + PLANE * d, frames)

    def earlier(d):
        return lax.rem(f + frames - PLANE * d, frames)

    def piece(ref, line):
        return ref.at[:, pl.ds(pl.multiple_of(line * width, 128), width)]

    barrier = pltpu.get_barrier_semaphore()
    for d in range(1, LINE):
        pl.semaphore_signal(barrier, inc=1, device_id={"frame": later(d)}, device_id_type=MESH)
    for peer in (to_x, to_y, to_pair):
        pl.semaphore_signal(barrier, inc=1, device_id=peer, device_id_type=MESH)
    pl.semaphore_wait(barrier, LINE + 2)

    sends = []
    pair = remote(part_ref.at[1 - hd], mpart, ms.at[0], mr.at[0], to_pair)
    pair.start()
    sends.append(pair)
    bufs = (kbuf, vbuf)
    own = []
    for i, (src, dst) in enumerate(
        ((k_ref, kbuf.at[f]), (v_ref, vbuf.at[f]), (q_ref, qbuf.at[z]))
    ):
        copy = pltpu.make_async_copy(piece(src, z), dst, own_sem.at[i])
        copy.start()
        own.append(copy)
    for i, src in enumerate((k_ref, v_ref, q_ref)):
        for d in (1, 3, 2):
            peer = later(d)
            dst = qbuf.at[z] if i == 2 else bufs[i].at[f]
            n = i * 3 + d - 1
            copy = remote(piece(src, lax.div(peer, PLANE)), dst, zs.at[n], zr.at[n], {"frame": peer})
            copy.start()
            sends.append(copy)

    def first(n):
        d, b = ORDER[n]
        at = earlier(d)
        block = bufs[b].at[at]
        if d == 0:
            own[b].wait()
        else:
            m = b * 3 + d - 1
            remote(block, block, zs.at[m], zr.at[m], {"frame": at}).wait_recv()
        for s, r, peer in ((xs, xr, to_x), (ys, yr, to_y)):
            copy = remote(block, block, s.at[n], r.at[n], peer)
            copy.start()
            sends.append(copy)

    def second(n):
        d, b = ORDER[n]
        at = earlier(d)
        block = bufs[b].at[at + step_x]
        remote(block, block, xs.at[n], xr.at[n], to_x).wait_recv()
        part = block.at[pl.ds(half, half)]
        copy = remote(part, part, dys.at[n], dyr.at[n], to_y)
        copy.start()
        sends.append(copy)
        block = bufs[b].at[at + step_y]
        remote(block, block, ys.at[n], yr.at[n], to_y).wait_recv()
        part = block.at[pl.ds(0, half)]
        copy = remote(part, part, dxs.at[n], dxr.at[n], to_x)
        copy.start()
        sends.append(copy)

    def third(n):
        d, b = ORDER[n]
        block = bufs[b].at[earlier(d) + step_x + step_y]
        part = block.at[pl.ds(0, half)]
        remote(part, part, dxs.at[n], dxr.at[n], to_x).wait_recv()
        part = block.at[pl.ds(half, half)]
        remote(part, part, dys.at[n], dyr.at[n], to_y).wait_recv()

    for n in range(len(ORDER)):
        first(n)
        if n >= 1:
            second(n - 1)
        if n == 0:
            pair.wait_recv()
            macc[0] = part_ref[hd] + mpart[...]
            for d in range(1, LINE):
                copy = remote(macc.at[0], mline.at[d - 1], ms.at[d], mr.at[d], {"frame": later(d)})
                copy.start()
                sends.append(copy)
        if n == 2:
            for d in range(1, LINE):
                remote(macc.at[0], mline.at[d - 1], ms.at[d], mr.at[d], {"frame": earlier(d)}).wait_recv()
            macc[1] = macc[0] + mline[0] + mline[1] + mline[2]
            copy = remote(macc.at[1], mx, ms.at[4], mr.at[4], to_x)
            copy.start()
            sends.append(copy)
        if n == 4:
            remote(macc.at[1], mx, ms.at[4], mr.at[4], to_x).wait_recv()
            macc[2] = macc[1] + mx[...]
            copy = remote(macc.at[2], my, ms.at[5], mr.at[5], to_y)
            copy.start()
            sends.append(copy)
    second(len(ORDER) - 1)
    remote(macc.at[2], my, ms.at[5], mr.at[5], to_y).wait_recv()
    mod_ref[...] = macc[2] + my[...]
    own[2].wait()
    for d in range(1, LINE):
        block = qbuf.at[lax.div(earlier(d), PLANE)]
        remote(block, block, zs.at[5 + d], zr.at[5 + d], {"frame": earlier(d)}).wait_recv()
    for n in range(len(ORDER)):
        third(n)

    for h in range(width // HD):
        cols = slice(h * HD, (h + 1) * HD)

        def block_of(i, carry):
            keys = kbuf[:, :, cols].reshape(frames * rows, HD)
            values = vbuf[:, :, cols].reshape(frames * rows, HD)
            scores = lax.dot_general(
                qbuf[i, :, cols], keys, (((1,), (1,)), ((), ())), preferred_element_type=jnp.float32
            ) * (1.0 / math.sqrt(HD))
            weights = jnp.exp(scores - jnp.max(scores, axis=1, keepdims=True))
            total = jnp.sum(weights, axis=1, keepdims=True)
            summed = jnp.dot(weights.astype(jnp.bfloat16), values, preferred_element_type=jnp.float32)
            obuf[i, :, cols] = (summed / total).astype(jnp.bfloat16)
            return carry

        lax.fori_loop(0, LINE, block_of, 0)
        for d in range(1, LINE):
            n = h * 3 + d - 1
            copy = remote(
                obuf.at[lax.div(later(d), PLANE), :, cols], arecv.at[z, :, cols],
                os.at[n], orr.at[n], {"frame": later(d)},
            )
            copy.start()
            sends.append(copy)
        arecv[z, :, cols] = obuf[z, :, cols]
    for h in range(width // HD):
        cols = slice(h * HD, (h + 1) * HD)
        for d in range(1, LINE):
            n = h * 3 + d - 1
            block = arecv.at[lax.div(earlier(d), PLANE), :, cols]
            remote(block, block, os.at[n], orr.at[n], {"frame": earlier(d)}).wait_recv()
    for j in range(LINE):
        attn_ref[:, j * width : (j + 1) * width] = arecv[j]
    for copy in sends:
        copy.wait_send()


def attend(queries, keys, values, part):
    rows, cols = queries.shape
    width = cols // LINE
    heads_sub = width // HD
    half_mod = part.shape[1:]
    bf, f32 = jnp.bfloat16, jnp.float32
    dma = pltpu.SemaphoreType.DMA
    spec = pl.BlockSpec(memory_space=pltpu.VMEM)
    blocks = LINE * PLANE
    count = len(ORDER)
    return pl.pallas_call(
        attend_kernel,
        out_shape=(jax.ShapeDtypeStruct((rows, cols), bf), jax.ShapeDtypeStruct(half_mod, f32)),
        in_specs=[spec] * 4,
        out_specs=(spec, spec),
        scratch_shapes=[
            pltpu.VMEM((blocks, rows, width), bf),
            pltpu.VMEM((blocks, rows, width), bf),
            pltpu.VMEM((LINE, rows, width), bf),
            pltpu.VMEM((LINE, rows, width), bf),
            pltpu.VMEM((LINE, rows, width), bf),
            pltpu.VMEM(half_mod, f32),
            pltpu.VMEM((3,) + half_mod, f32),
            pltpu.VMEM((LINE - 1,) + half_mod, f32),
            pltpu.VMEM(half_mod, f32),
            pltpu.VMEM(half_mod, f32),
            dma((3,)), dma((9,)), dma((9,)),
        ]
        + [dma((count,))] * 8
        + [dma((3 * heads_sub,))] * 2
        + [dma((6,))] * 2,
        compiler_params=pltpu.CompilerParams(
            collective_id=0, has_side_effects=True, vmem_limit_bytes=40 * 1024 * 1024
        ),
    )(queries, keys, values, part)


def accumulate(carry, queries, keys_block, values_block):
    count = keys_block.shape[0]
    heads_here = queries.shape[1]
    keys_three = keys_block.reshape(count, heads_here, HD)
    values_three = values_block.reshape(count, heads_here, HD).astype(jnp.float32)
    scores = jnp.einsum("thd,shd->ths", queries, keys_three, preferred_element_type=jnp.float32) * (
        1.0 / math.sqrt(HD)
    )
    top_old, total_old, summed = carry
    top_new = jnp.maximum(top_old, jnp.max(scores, axis=2))
    weights = jnp.exp(scores - top_new[:, :, None])
    total_new = jnp.sum(weights, axis=2)
    summed_new = jnp.einsum("ths,shd->thd", weights, values_three, precision=lax.Precision.HIGHEST)
    return (top_new, total_new, summed_new)


def shards(
    residual,
    query_proj,
    key_proj,
    value_proj,
    q_gain,
    k_gain,
    time_embed,
    time_proj,
    mod_table,
    out_weight,
):
    emb = jax.nn.silu(time_embed)
    partial_mod = jnp.einsum(
        "r,rcd->cd", emb, time_proj.astype(jnp.float32), precision=lax.Precision.HIGHEST
    )
    width = mod_table.shape[1]
    groups = lax.axis_size("head")
    place = lax.axis_index("head")
    tok_rows = query_proj.shape[0]
    heads_here = query_proj.shape[1] // HD
    query_wide = query_proj.astype(jnp.float32)
    key_wide = key_proj.astype(jnp.float32)
    total_q, total_k = lax.psum(
        (jnp.sum(query_wide * query_wide, axis=1), jnp.sum(key_wide * key_wide, axis=1)), "head"
    )
    query_rms = lax.rsqrt(total_q / (HEADS * HD) + 1e-06)
    key_rms = lax.rsqrt(total_k / (HEADS * HD) + 1e-06)
    queries = (query_wide * query_rms[:, None] * q_gain).astype(jnp.bfloat16)
    keys = (key_wide * key_rms[:, None] * k_gain).astype(jnp.bfloat16)
    fused = groups == 2 and lax.axis_size("frame") == LINE * PLANE and heads_here % LINE == 0
    if fused:
        part = partial_mod.reshape(3, groups, width).transpose(1, 0, 2)
        attn, share = attend(queries, keys, value_proj, part)
    else:
        summed_mod = lax.psum(partial_mod, ("frame", "head"))
        share = lax.dynamic_slice_in_dim(summed_mod, place * width, width, 1)
        start_state = (
            jnp.full((tok_rows, heads_here), -1e30, jnp.float32),
            jnp.zeros((tok_rows, heads_here), jnp.float32),
            jnp.zeros((tok_rows, heads_here, HD), jnp.float32),
        )
        top_final, total_final, summed_final = accumulate(
            start_state,
            queries.reshape(tok_rows, heads_here, HD),
            lax.all_gather(keys, "frame", axis=0, tiled=True),
            lax.all_gather(value_proj, "frame", axis=0, tiled=True),
        )
        attn = (
            (summed_final / total_final[:, :, None])
            .astype(jnp.bfloat16)
            .reshape(tok_rows, heads_here * HD)
        )
    modulation = mod_table + share
    gate = modulation[0]
    shift = modulation[1]
    scale = modulation[2]
    if fused:
        full = jnp.dot(attn, out_weight, preferred_element_type=jnp.float32)
        mine = lax.dynamic_slice_in_dim(full, place * width, width, 1)
        other = lax.dynamic_slice_in_dim(full, (1 - place) * width, width, 1).astype(jnp.bfloat16)
        proj = mine + lax.ppermute(other, "head", [(0, 1), (1, 0)]).astype(jnp.float32)
    else:
        proj = (
            lax.psum_scatter(
                lax.dot_general(
                    out_weight, attn, (((0,), (1,)), ((), ())), preferred_element_type=jnp.float32
                ).astype(jnp.bfloat16),
                "head",
                scatter_dimension=0,
                tiled=True,
            )
            .astype(jnp.float32)
            .T
        )
    hidden_out = (residual.astype(jnp.float32) + gate * proj).astype(jnp.bfloat16)
    hidden32 = lax.optimization_barrier(hidden_out).astype(jnp.float32)
    row_sum, row_squares = lax.psum(
        (jnp.sum(hidden32, axis=1), jnp.sum(hidden32 * hidden32, axis=1)), "head"
    )
    mean = row_sum[:, None] / D
    var = row_squares[:, None] / D - mean * mean
    mlp_input = ((hidden32 - mean) * lax.rsqrt(var + 1e-06) * (1.0 + scale) + shift).astype(
        jnp.bfloat16
    )
    return (hidden_out, mlp_input)


def solution(mesh):
    in_specs = (
        P("frame", "head"),
        P("frame", "head"),
        P("frame", "head"),
        P("frame", "head"),
        P("head"),
        P("head"),
        P(("frame", "head")),
        P(("frame", "head"), None, None),
        P(None, "head"),
        P("head", None),
    )
    out_specs = (P("frame", "head"), P("frame", "head"))
    return jax.shard_map(shards, mesh=mesh, in_specs=in_specs, out_specs=out_specs, check_vma=False)
```

```python
import math

import jax
import jax.numpy as jnp
from jax import lax
from jax.experimental import pallas as pl
from jax.experimental.pallas import tpu as pltpu
from jax.sharding import PartitionSpec as P

D = 5120
HEADS = 24
HD = 128


MESH = pl.DeviceIdType.MESH
PLANE = 4
LINE = 4
ORDER = ((0, 1), (0, 0), (1, 1), (3, 1), (2, 1), (1, 0), (3, 0), (2, 0))
INDEX = {pair: n for n, pair in enumerate(ORDER)}
TILE = 512
WEIGHT_PARTS = 4


def remote(src, dst, send, recv, device):
    return pltpu.make_async_remote_copy(
        src_ref=src, dst_ref=dst, send_sem=send, recv_sem=recv, device_id=device, device_id_type=MESH
    )


def block_kernel(
    q_ref, k_ref, v_hbm, qg_ref, kg_ref, te_ref, table_ref, res_hbm, proj_hbm, weight_hbm,
    hidden_ref, mlp_ref,
    qn, kn, kbuf, vbuf, qbuf, obuf, arecv, attn, top, total, summed,
    squares, squares_in, part, mpart, macc, mline, mx, my, tbuf, wbuf, rbuf, pout, pin, stat, stat_in,
    own_sem, load_sem, zs, zr, xs, xr, ys, yr, dxs, dxr, dys, dyr, os, orr, ms, mr, ps, pr, ss, sr,
):
    f32, bf = jnp.float32, jnp.bfloat16
    frames = LINE * PLANE
    f = lax.axis_index("frame")
    hd = lax.axis_index("head")
    z = lax.div(f, PLANE)
    x = lax.rem(f, 2)
    y = lax.rem(lax.div(f, 2), 2)
    step_x = 1 - 2 * x
    step_y = 2 - 4 * y
    to_x = {"frame": f + step_x}
    to_y = {"frame": f + step_y}
    to_pair = {"head": 1 - hd}
    rows, cols_all = q_ref.shape
    half = rows // 2
    width = cols_all // LINE
    heads_sub = width // HD
    owned = hidden_ref.shape[1]

    def later(d):
        return lax.rem(f + PLANE * d, frames)

    def earlier(d):
        return lax.rem(f + frames - PLANE * d, frames)

    def piece(ref, line):
        return ref.at[:, pl.ds(pl.multiple_of(line * width, 128), width)]

    sends = []

    def send(src, dst, s, r, peer):
        copy = remote(src, dst, s, r, peer)
        copy.start()
        sends.append(copy)

    loads = [pltpu.make_async_copy(proj_hbm, tbuf, load_sem.at[0])]
    depth = cols_all // WEIGHT_PARTS
    for i in range(WEIGHT_PARTS):
        at = pl.ds(i * depth, depth)
        loads.append(pltpu.make_async_copy(weight_hbm.at[at], wbuf.at[at], load_sem.at[1 + i]))
    loads.append(pltpu.make_async_copy(res_hbm, rbuf, load_sem.at[1 + WEIGHT_PARTS]))

    barrier = pltpu.get_barrier_semaphore()
    for d in range(1, LINE):
        pl.semaphore_signal(barrier, inc=1, device_id={"frame": later(d)}, device_id_type=MESH)
    for peer in (to_x, to_y, to_pair):
        pl.semaphore_signal(barrier, inc=1, device_id=peer, device_id_type=MESH)

    for i, ref in enumerate((q_ref, k_ref)):
        lanes = jnp.zeros((rows, 128), f32)
        for c in range(0, cols_all, 128):
            wide = ref[:, c : c + 128].astype(f32)
            lanes += wide * wide
        squares[i] = lanes
    pl.semaphore_wait(barrier, LINE + 2)

    bufs = (kbuf, vbuf)
    own_v = pltpu.make_async_copy(piece(v_hbm, z), vbuf.at[f], own_sem.at[1])
    own_v.start()
    send(squares, squares_in, ss.at[0], sr.at[0], to_pair)

    def send_line(i, src, dst):
        for d in (1, 3, 2):
            peer = later(d)
            n = i * 3 + d - 1
            send(piece(src, lax.div(peer, PLANE)), dst, zs.at[n], zr.at[n], {"frame": peer})

    send_line(1, v_hbm, vbuf.at[f])
    for copy in loads:
        copy.start()

    remote(squares, squares_in, ss.at[0], sr.at[0], to_pair).wait_recv()
    for i, (ref, gain, out) in enumerate(((q_ref, qg_ref, qn), (k_ref, kg_ref, kn))):
        sums = jnp.sum(squares[i] + squares_in[i], axis=1, keepdims=True)
        rms = lax.rsqrt(sums / (HEADS * HD) + 1e-06)
        for c in range(0, cols_all, 128):
            at = slice(c, c + 128)
            out[:, at] = (ref[:, at].astype(f32) * rms * gain[:, at]).astype(bf)
    send_line(2, qn, qbuf.at[z])
    send_line(0, kn, kbuf.at[f])
    own_q = pltpu.make_async_copy(piece(qn, z), qbuf.at[z], own_sem.at[2])
    own_q.start()
    own_k = pltpu.make_async_copy(piece(kn, z), kbuf.at[f], own_sem.at[0])
    own_k.start()
    own = (own_k, own_v)

    def first(d, b):
        n = INDEX[d, b]
        at = earlier(d)
        block = bufs[b].at[at]
        if d == 0:
            own[b].wait()
        else:
            m = b * 3 + d - 1
            remote(block, block, zs.at[m], zr.at[m], {"frame": at}).wait_recv()
        send(block, block, xs.at[n], xr.at[n], to_x)
        send(block, block, ys.at[n], yr.at[n], to_y)

    def second(d, b):
        n = INDEX[d, b]
        at = earlier(d)
        block = bufs[b].at[at + step_x]
        remote(block, block, xs.at[n], xr.at[n], to_x).wait_recv()
        low = block.at[pl.ds(half, half)]
        send(low, low, dys.at[n], dyr.at[n], to_y)
        block = bufs[b].at[at + step_y]
        remote(block, block, ys.at[n], yr.at[n], to_y).wait_recv()
        high = block.at[pl.ds(0, half)]
        send(high, high, dxs.at[n], dxr.at[n], to_x)

    def third(d, b):
        n = INDEX[d, b]
        block = bufs[b].at[earlier(d) + step_x + step_y]
        high = block.at[pl.ds(0, half)]
        remote(high, high, dxs.at[n], dxr.at[n], to_x).wait_recv()
        low = block.at[pl.ds(half, half)]
        remote(low, low, dys.at[n], dyr.at[n], to_y).wait_recv()

    def absorb(d, opening, closing):
        base = pl.multiple_of(lax.div(earlier(d), PLANE) * PLANE, PLANE)
        group = pl.ds(base, PLANE)
        for h in range(heads_sub):
            cols = slice(h * HD, (h + 1) * HD)

            def block_of(i, carry):
                keys = kbuf[group, :, cols].reshape(PLANE * rows, HD)
                values = vbuf[group, :, cols].reshape(PLANE * rows, HD)
                scores = lax.dot_general(
                    qbuf[i, :, cols], keys, (((1,), (1,)), ((), ())), preferred_element_type=f32
                ) * (1.0 / math.sqrt(HD))
                peak = jnp.max(scores, axis=1, keepdims=True)
                if not opening:
                    old = top[h, i]
                    peak = jnp.maximum(old, peak)
                    fade = jnp.exp(old - peak)
                weights = jnp.exp(scores - peak)
                count = jnp.sum(weights, axis=1, keepdims=True)
                mixed = jnp.dot(weights.astype(bf), values, preferred_element_type=f32)
                if not opening:
                    count = count + fade * total[h, i]
                    mixed = mixed + fade * summed[h, i]
                if closing:
                    obuf[i, :, cols] = (mixed / count).astype(bf)
                else:
                    top[h, i] = peak
                    total[h, i] = count
                    summed[h, i] = mixed
                return carry

            lax.fori_loop(0, LINE, block_of, 0)
            if closing:
                for e in range(1, LINE):
                    n = h * 3 + e - 1
                    send(
                        obuf.at[lax.div(later(e), PLANE), :, cols], arecv.at[z, :, cols],
                        os.at[n], orr.at[n], {"frame": later(e)},
                    )
                arecv[z, :, cols] = obuf[z, :, cols]

    first(0, 1)
    first(0, 0)
    second(0, 1)
    loads[0].wait()
    t = te_ref[...]
    emb = t / (1.0 + jnp.exp(-t))
    high = emb.astype(bf).astype(f32)
    middle = (emb - high).astype(bf).astype(f32)
    low = emb - high - middle
    row = lax.broadcasted_iota(jnp.int32, (8, emb.shape[1]), 0)
    split = jnp.where(row == 0, high, jnp.where(row == 1, middle, jnp.where(row == 2, low, 0.0)))
    split = split.astype(bf)
    for c in range(3):
        for side in range(2):
            term = jnp.dot(
                split, tbuf[c, :, side * owned : (side + 1) * owned], preferred_element_type=f32
            )
            part[side, c : c + 1, :] = jnp.sum(term, axis=0, keepdims=True)
    send(part.at[1 - hd], mpart, ms.at[0], mr.at[0], to_pair)
    second(0, 0)
    first(1, 1)
    first(3, 1)
    remote(part.at[1 - hd], mpart, ms.at[0], mr.at[0], to_pair).wait_recv()
    macc[0] = part[hd] + mpart[...]
    for d in range(1, LINE):
        send(macc.at[0], mline.at[d - 1], ms.at[d], mr.at[d], {"frame": later(d)})
    second(1, 1)
    first(2, 1)
    second(3, 1)
    own_q.wait()
    for d in range(1, LINE):
        block = qbuf.at[lax.div(earlier(d), PLANE)]
        remote(block, block, zs.at[5 + d], zr.at[5 + d], {"frame": earlier(d)}).wait_recv()
    second(2, 1)
    third(0, 1)
    third(0, 0)
    absorb(0, True, False)
    first(1, 0)
    first(3, 0)
    second(1, 0)
    for d in range(1, LINE):
        remote(macc.at[0], mline.at[d - 1], ms.at[d], mr.at[d], {"frame": earlier(d)}).wait_recv()
    macc[1] = macc[0] + mline[0] + mline[1] + mline[2]
    send(macc.at[1], mx, ms.at[4], mr.at[4], to_x)
    first(2, 0)
    second(3, 0)
    third(1, 1)
    third(1, 0)
    absorb(1, False, False)
    second(2, 0)
    remote(macc.at[1], mx, ms.at[4], mr.at[4], to_x).wait_recv()
    macc[2] = macc[1] + mx[...]
    send(macc.at[2], my, ms.at[5], mr.at[5], to_y)
    third(3, 1)
    third(3, 0)
    absorb(3, False, False)
    third(2, 1)
    third(2, 0)
    absorb(2, False, True)

    remote(macc.at[2], my, ms.at[5], mr.at[5], to_y).wait_recv()
    macc[3] = macc[2] + my[...] + table_ref[...]
    for copy in loads[1:]:
        copy.wait()
    for h in range(heads_sub):
        cols = slice(h * HD, (h + 1) * HD)
        for d in range(1, LINE):
            n = h * 3 + d - 1
            block = arecv.at[lax.div(earlier(d), PLANE), :, cols]
            remote(block, block, os.at[n], orr.at[n], {"frame": earlier(d)}).wait_recv()
    for j in range(LINE):
        attn[:, j * width : (j + 1) * width] = arecv[j]

    def project(side, at):
        begin = pl.multiple_of(side * owned + at, 128)
        return jnp.dot(attn[...], wbuf[:, pl.ds(begin, TILE)], preferred_element_type=f32)

    for i in range(owned // TILE):
        at = slice(i * TILE, (i + 1) * TILE)
        pout[:, at] = project(1 - hd, i * TILE).astype(bf)
        send(pout.at[:, at], pin.at[:, at], ps.at[i], pr.at[i], to_pair)
    sum_lanes = jnp.zeros((rows, 128), f32)
    square_lanes = jnp.zeros((rows, 128), f32)
    for i in range(owned // TILE):
        at = slice(i * TILE, (i + 1) * TILE)
        mine = project(hd, i * TILE)
        remote(pout.at[:, at], pin.at[:, at], ps.at[i], pr.at[i], to_pair).wait_recv()
        mine = mine + pin[:, at].astype(f32)
        hidden = (rbuf[:, at].astype(f32) + macc[3, 0:1, at] * mine).astype(bf)
        hidden_ref[:, at] = hidden
        wide = hidden.astype(f32)
        for c in range(0, TILE, 128):
            lane = wide[:, c : c + 128]
            sum_lanes += lane
            square_lanes += lane * lane
    stat[0] = sum_lanes
    stat[1] = square_lanes
    send(stat, stat_in, ss.at[1], sr.at[1], to_pair)
    remote(stat, stat_in, ss.at[1], sr.at[1], to_pair).wait_recv()
    mean = jnp.sum(stat[0] + stat_in[0], axis=1, keepdims=True) / D
    var = jnp.sum(stat[1] + stat_in[1], axis=1, keepdims=True) / D - mean * mean
    spread = lax.rsqrt(var + 1e-06)
    for i in range(owned // TILE):
        at = slice(i * TILE, (i + 1) * TILE)
        wide = hidden_ref[:, at].astype(f32)
        mlp_ref[:, at] = (
            (wide - mean) * spread * (1.0 + macc[3, 2:3, at]) + macc[3, 1:2, at]
        ).astype(bf)
    for copy in sends:
        copy.wait_send()


def fused_block(
    residual, query_proj, key_proj, value_proj, q_gain, k_gain, time_embed, time_proj, mod_table, out_weight
):
    rows, cols = query_proj.shape
    width = cols // LINE
    heads_sub = width // HD
    owned = residual.shape[1]
    half_mod = mod_table.shape
    bf, f32 = jnp.bfloat16, jnp.float32
    dma = pltpu.SemaphoreType.DMA
    vmem = pl.BlockSpec(memory_space=pltpu.VMEM)
    hbm = pl.BlockSpec(memory_space=pl.ANY)
    blocks = LINE * PLANE
    count = len(ORDER)
    lines = time_proj.transpose(1, 0, 2)
    out = jax.ShapeDtypeStruct((rows, owned), bf)
    slab = pltpu.VMEM((LINE, rows, width), bf)
    lanes = pltpu.VMEM((2, rows, 128), f32)
    column = pltpu.VMEM((heads_sub, LINE, rows, 1), f32)
    return pl.pallas_call(
        block_kernel,
        out_shape=(out, out),
        in_specs=[vmem, vmem, hbm, vmem, vmem, vmem, vmem, hbm, hbm, hbm],
        out_specs=(vmem, vmem),
        scratch_shapes=[
            pltpu.VMEM((rows, cols), bf),
            pltpu.VMEM((rows, cols), bf),
            pltpu.VMEM((blocks, rows, width), bf),
            pltpu.VMEM((blocks, rows, width), bf),
            slab, slab, slab,
            pltpu.VMEM((rows, cols), bf),
            column, column,
            pltpu.VMEM((heads_sub, LINE, rows, HD), f32),
            lanes, lanes,
            pltpu.VMEM((2,) + half_mod, f32),
            pltpu.VMEM(half_mod, f32),
            pltpu.VMEM((4,) + half_mod, f32),
            pltpu.VMEM((LINE - 1,) + half_mod, f32),
            pltpu.VMEM(half_mod, f32),
            pltpu.VMEM(half_mod, f32),
            pltpu.VMEM(lines.shape, bf),
            pltpu.VMEM(out_weight.shape, bf),
            pltpu.VMEM((rows, owned), bf),
            pltpu.VMEM((rows, owned), bf),
            pltpu.VMEM((rows, owned), bf),
            lanes, lanes,
            dma((3,)), dma((2 + WEIGHT_PARTS,)), dma((9,)), dma((9,)),
        ]
        + [dma((count,))] * 8
        + [dma((3 * heads_sub,))] * 2
        + [dma((6,))] * 2
        + [dma((owned // TILE,))] * 2
        + [dma((2,))] * 2,
        compiler_params=pltpu.CompilerParams(
            collective_id=0, has_side_effects=True, vmem_limit_bytes=60 * 1024 * 1024
        ),
    )(
        query_proj, key_proj, value_proj, q_gain.reshape(1, cols), k_gain.reshape(1, cols),
        time_embed.reshape(1, -1), mod_table, residual, lines, out_weight,
    )


def accumulate(carry, queries, keys_block, values_block):
    count = keys_block.shape[0]
    heads_here = queries.shape[1]
    keys_three = keys_block.reshape(count, heads_here, HD)
    values_three = values_block.reshape(count, heads_here, HD).astype(jnp.float32)
    scores = jnp.einsum("thd,shd->ths", queries, keys_three, preferred_element_type=jnp.float32) * (
        1.0 / math.sqrt(HD)
    )
    top_old, total_old, summed = carry
    top_new = jnp.maximum(top_old, jnp.max(scores, axis=2))
    weights = jnp.exp(scores - top_new[:, :, None])
    total_new = jnp.sum(weights, axis=2)
    summed_new = jnp.einsum("ths,shd->thd", weights, values_three, precision=lax.Precision.HIGHEST)
    return (top_new, total_new, summed_new)


def shards(
    residual,
    query_proj,
    key_proj,
    value_proj,
    q_gain,
    k_gain,
    time_embed,
    time_proj,
    mod_table,
    out_weight,
):
    if (
        lax.axis_size("head") == 2
        and lax.axis_size("frame") == LINE * PLANE
        and query_proj.shape[1] % (LINE * HD) == 0
    ):
        return fused_block(
            residual, query_proj, key_proj, value_proj, q_gain, k_gain, time_embed, time_proj, mod_table, out_weight
        )
    emb = jax.nn.silu(time_embed)
    partial_mod = jnp.einsum(
        "r,rcd->cd", emb, time_proj.astype(jnp.float32), precision=lax.Precision.HIGHEST
    )
    width = mod_table.shape[1]
    summed_mod = lax.psum(partial_mod, ("frame", "head"))
    share = lax.dynamic_slice_in_dim(summed_mod, lax.axis_index("head") * width, width, 1)
    modulation = mod_table + share
    gate = modulation[0]
    shift = modulation[1]
    scale = modulation[2]
    tok_rows = query_proj.shape[0]
    heads_here = query_proj.shape[1] // HD
    query_wide = query_proj.astype(jnp.float32)
    key_wide = key_proj.astype(jnp.float32)
    total_q, total_k = lax.psum(
        (jnp.sum(query_wide * query_wide, axis=1), jnp.sum(key_wide * key_wide, axis=1)), "head"
    )
    query_rms = lax.rsqrt(total_q / (HEADS * HD) + 1e-06)
    key_rms = lax.rsqrt(total_k / (HEADS * HD) + 1e-06)
    queries = (
        (query_wide * query_rms[:, None] * q_gain)
        .astype(jnp.bfloat16)
        .reshape(tok_rows, heads_here, HD)
    )
    start_state = (
        jnp.full((tok_rows, heads_here), -1e30, jnp.float32),
        jnp.zeros((tok_rows, heads_here), jnp.float32),
        jnp.zeros((tok_rows, heads_here, HD), jnp.float32),
    )
    every_scale = lax.all_gather(key_rms, "frame", axis=0, tiled=True)
    keys_block = (
        lax.all_gather(key_proj, "frame", axis=0, tiled=True).astype(jnp.float32)
        * every_scale[:, None]
        * k_gain
    ).astype(jnp.bfloat16)
    top_final, total_final, summed_final = accumulate(
        start_state, queries, keys_block, lax.all_gather(value_proj, "frame", axis=0, tiled=True)
    )
    attn = (
        (summed_final / total_final[:, :, None])
        .astype(jnp.bfloat16)
        .reshape(tok_rows, heads_here * HD)
    )
    proj = (
        lax.psum_scatter(
            lax.dot_general(
                out_weight, attn, (((0,), (1,)), ((), ())), preferred_element_type=jnp.float32
            ).astype(jnp.bfloat16),
            "head",
            scatter_dimension=0,
            tiled=True,
        )
        .astype(jnp.float32)
        .T
    )
    hidden_out = (residual.astype(jnp.float32) + gate * proj).astype(jnp.bfloat16)
    hidden32 = lax.optimization_barrier(hidden_out).astype(jnp.float32)
    row_sum, row_squares = lax.psum(
        (jnp.sum(hidden32, axis=1), jnp.sum(hidden32 * hidden32, axis=1)), "head"
    )
    mean = row_sum[:, None] / D
    var = row_squares[:, None] / D - mean * mean
    mlp_input = ((hidden32 - mean) * lax.rsqrt(var + 1e-06) * (1.0 + scale) + shift).astype(
        jnp.bfloat16
    )
    return (hidden_out, mlp_input)


def solution(mesh):
    in_specs = (
        P("frame", "head"),
        P("frame", "head"),
        P("frame", "head"),
        P("frame", "head"),
        P("head"),
        P("head"),
        P(("frame", "head")),
        P(("frame", "head"), None, None),
        P(None, "head"),
        P("head", None),
    )
    out_specs = (P("frame", "head"), P("frame", "head"))
    return jax.shard_map(shards, mesh=mesh, in_specs=in_specs, out_specs=out_specs, check_vma=False)
```

```python
import math

import jax
import jax.numpy as jnp
from jax import lax
from jax.experimental import pallas as pl
from jax.experimental.pallas import tpu as pltpu
from jax.sharding import PartitionSpec as P

D = 5120
HEADS = 24
HD = 128


MESH = pl.DeviceIdType.MESH
PLANE = 4
LINE = 4
ORDER = ((0, 1), (0, 0), (1, 1), (3, 1), (2, 1), (1, 0), (3, 0), (2, 0))
INDEX = {pair: n for n, pair in enumerate(ORDER)}
TILE = 512
WEIGHT_PARTS = 4


def remote(src, dst, send, recv, device):
    return pltpu.make_async_remote_copy(
        src_ref=src, dst_ref=dst, send_sem=send, recv_sem=recv, device_id=device, device_id_type=MESH
    )


def block_kernel(
    q_ref, k_ref, v_hbm, qg_ref, kg_ref, te_ref, table_ref, res_hbm, proj_hbm, weight_hbm,
    hidden_ref, row_ref, mod_ref,
    qn, kn, kbuf, vbuf, qbuf, obuf, arecv, attn, top, total, summed,
    squares, squares_in, part, mpart, macc, mline, mx, my, tbuf, wbuf, rbuf, pout, pin, stat, stat_in,
    own_sem, load_sem, zs, zr, xs, xr, ys, yr, dxs, dxr, dys, dyr, os, orr, ms, mr, ps, pr, ss, sr,
):
    f32, bf = jnp.float32, jnp.bfloat16
    frames = LINE * PLANE
    f = lax.axis_index("frame")
    hd = lax.axis_index("head")
    z = lax.div(f, PLANE)
    x = lax.rem(f, 2)
    y = lax.rem(lax.div(f, 2), 2)
    step_x = 1 - 2 * x
    step_y = 2 - 4 * y
    to_x = {"frame": f + step_x}
    to_y = {"frame": f + step_y}
    to_pair = {"head": 1 - hd}
    rows, cols_all = q_ref.shape
    half = rows // 2
    width = cols_all // LINE
    heads_sub = width // HD
    owned = hidden_ref.shape[1]

    def later(d):
        return lax.rem(f + PLANE * d, frames)

    def earlier(d):
        return lax.rem(f + frames - PLANE * d, frames)

    def piece(ref, line):
        return ref.at[:, pl.ds(pl.multiple_of(line * width, 128), width)]

    sends = []

    def send(src, dst, s, r, peer):
        copy = remote(src, dst, s, r, peer)
        copy.start()
        sends.append(copy)

    loads = [pltpu.make_async_copy(proj_hbm, tbuf, load_sem.at[0])]
    depth = cols_all // WEIGHT_PARTS
    for i in range(WEIGHT_PARTS):
        at = pl.ds(i * depth, depth)
        loads.append(pltpu.make_async_copy(weight_hbm.at[at], wbuf.at[at], load_sem.at[1 + i]))
    loads.append(pltpu.make_async_copy(res_hbm, rbuf, load_sem.at[1 + WEIGHT_PARTS]))

    barrier = pltpu.get_barrier_semaphore()
    for d in range(1, LINE):
        pl.semaphore_signal(barrier, inc=1, device_id={"frame": later(d)}, device_id_type=MESH)
    for peer in (to_x, to_y, to_pair):
        pl.semaphore_signal(barrier, inc=1, device_id=peer, device_id_type=MESH)

    for i, ref in enumerate((q_ref, k_ref)):
        lanes = jnp.zeros((rows, 128), f32)
        for c in range(0, cols_all, 128):
            wide = ref[:, c : c + 128].astype(f32)
            lanes += wide * wide
        squares[i] = lanes
    pl.semaphore_wait(barrier, LINE + 2)

    bufs = (kbuf, vbuf)
    own_v = pltpu.make_async_copy(piece(v_hbm, z), vbuf.at[f], own_sem.at[1])
    own_v.start()
    send(squares, squares_in, ss.at[0], sr.at[0], to_pair)

    def send_line(i, src, dst):
        for d in (1, 3, 2):
            peer = later(d)
            n = i * 3 + d - 1
            send(piece(src, lax.div(peer, PLANE)), dst, zs.at[n], zr.at[n], {"frame": peer})

    send_line(1, v_hbm, vbuf.at[f])
    for copy in loads:
        copy.start()

    remote(squares, squares_in, ss.at[0], sr.at[0], to_pair).wait_recv()
    for i, (ref, gain, out) in enumerate(((q_ref, qg_ref, qn), (k_ref, kg_ref, kn))):
        sums = jnp.sum(squares[i] + squares_in[i], axis=1, keepdims=True)
        rms = lax.rsqrt(sums / (HEADS * HD) + 1e-06)
        for c in range(0, cols_all, 128):
            at = slice(c, c + 128)
            out[:, at] = (ref[:, at].astype(f32) * rms * gain[at].reshape(1, 128)).astype(bf)
    send_line(2, qn, qbuf.at[z])
    send_line(0, kn, kbuf.at[f])
    own_q = pltpu.make_async_copy(piece(qn, z), qbuf.at[z], own_sem.at[2])
    own_q.start()
    own_k = pltpu.make_async_copy(piece(kn, z), kbuf.at[f], own_sem.at[0])
    own_k.start()
    own = (own_k, own_v)

    def first(d, b):
        n = INDEX[d, b]
        at = earlier(d)
        block = bufs[b].at[at]
        if d == 0:
            own[b].wait()
        else:
            m = b * 3 + d - 1
            remote(block, block, zs.at[m], zr.at[m], {"frame": at}).wait_recv()
        send(block, block, xs.at[n], xr.at[n], to_x)
        send(block, block, ys.at[n], yr.at[n], to_y)

    def second(d, b):
        n = INDEX[d, b]
        at = earlier(d)
        block = bufs[b].at[at + step_x]
        remote(block, block, xs.at[n], xr.at[n], to_x).wait_recv()
        low = block.at[pl.ds(half, half)]
        send(low, low, dys.at[n], dyr.at[n], to_y)
        block = bufs[b].at[at + step_y]
        remote(block, block, ys.at[n], yr.at[n], to_y).wait_recv()
        high = block.at[pl.ds(0, half)]
        send(high, high, dxs.at[n], dxr.at[n], to_x)

    def third(d, b):
        n = INDEX[d, b]
        block = bufs[b].at[earlier(d) + step_x + step_y]
        high = block.at[pl.ds(0, half)]
        remote(high, high, dxs.at[n], dxr.at[n], to_x).wait_recv()
        low = block.at[pl.ds(half, half)]
        remote(low, low, dys.at[n], dyr.at[n], to_y).wait_recv()

    def absorb(d, opening, closing):
        base = pl.multiple_of(lax.div(earlier(d), PLANE) * PLANE, PLANE)
        group = pl.ds(base, PLANE)
        for h in range(heads_sub):
            cols = slice(h * HD, (h + 1) * HD)

            def block_of(i, carry):
                keys = kbuf[group, :, cols].reshape(PLANE * rows, HD)
                values = vbuf[group, :, cols].reshape(PLANE * rows, HD)
                scores = lax.dot_general(
                    qbuf[i, :, cols], keys, (((1,), (1,)), ((), ())), preferred_element_type=f32
                ) * (1.0 / math.sqrt(HD))
                peak = jnp.max(scores, axis=1, keepdims=True)
                if not opening:
                    old = top[h, i]
                    peak = jnp.maximum(old, peak)
                    fade = jnp.exp(old - peak)
                weights = jnp.exp(scores - peak)
                count = jnp.sum(weights, axis=1, keepdims=True)
                mixed = jnp.dot(weights.astype(bf), values, preferred_element_type=f32)
                if not opening:
                    count = count + fade * total[h, i]
                    mixed = mixed + fade * summed[h, i]
                if closing:
                    obuf[i, :, cols] = (mixed / count).astype(bf)
                else:
                    top[h, i] = peak
                    total[h, i] = count
                    summed[h, i] = mixed
                return carry

            lax.fori_loop(0, LINE, block_of, 0, unroll=True)
            if closing:
                for e in range(1, LINE):
                    n = h * 3 + e - 1
                    send(
                        obuf.at[lax.div(later(e), PLANE), :, cols], arecv.at[z, :, cols],
                        os.at[n], orr.at[n], {"frame": later(e)},
                    )
                arecv[z, :, cols] = obuf[z, :, cols]

    first(0, 1)
    first(0, 0)
    second(0, 1)
    loads[0].wait()
    t = te_ref[...]
    emb = t / (1.0 + jnp.exp(-t))
    high = emb.astype(bf).astype(f32)
    middle = (emb - high).astype(bf).astype(f32)
    low = emb - high - middle
    row = lax.broadcasted_iota(jnp.int32, (8, emb.shape[1]), 0)
    split = jnp.where(row == 0, high, jnp.where(row == 1, middle, jnp.where(row == 2, low, 0.0)))
    split = split.astype(bf)
    for c in range(3):
        for side in range(2):
            term = jnp.dot(
                split, tbuf[c, :, side * owned : (side + 1) * owned], preferred_element_type=f32
            )
            part[side, c : c + 1, :] = jnp.sum(term, axis=0, keepdims=True)
    send(part.at[1 - hd], mpart, ms.at[0], mr.at[0], to_pair)
    second(0, 0)
    first(1, 1)
    first(3, 1)
    remote(part.at[1 - hd], mpart, ms.at[0], mr.at[0], to_pair).wait_recv()
    macc[0] = part[hd] + mpart[...]
    for d in range(1, LINE):
        send(macc.at[0], mline.at[d - 1], ms.at[d], mr.at[d], {"frame": later(d)})
    second(1, 1)
    first(2, 1)
    second(3, 1)
    own_q.wait()
    for d in range(1, LINE):
        block = qbuf.at[lax.div(earlier(d), PLANE)]
        remote(block, block, zs.at[5 + d], zr.at[5 + d], {"frame": earlier(d)}).wait_recv()
    second(2, 1)
    third(0, 1)
    third(0, 0)
    absorb(0, True, False)
    first(1, 0)
    first(3, 0)
    second(1, 0)
    for d in range(1, LINE):
        remote(macc.at[0], mline.at[d - 1], ms.at[d], mr.at[d], {"frame": earlier(d)}).wait_recv()
    macc[1] = macc[0] + mline[0] + mline[1] + mline[2]
    send(macc.at[1], mx, ms.at[4], mr.at[4], to_x)
    first(2, 0)
    second(3, 0)
    third(1, 1)
    third(1, 0)
    absorb(1, False, False)
    second(2, 0)
    remote(macc.at[1], mx, ms.at[4], mr.at[4], to_x).wait_recv()
    macc[2] = macc[1] + mx[...]
    send(macc.at[2], my, ms.at[5], mr.at[5], to_y)
    third(3, 1)
    third(3, 0)
    absorb(3, False, False)
    third(2, 1)
    third(2, 0)
    absorb(2, False, True)

    remote(macc.at[2], my, ms.at[5], mr.at[5], to_y).wait_recv()
    macc[3] = macc[2] + my[...] + table_ref[...]
    for copy in loads[1:]:
        copy.wait()
    for h in range(heads_sub):
        cols = slice(h * HD, (h + 1) * HD)
        for d in range(1, LINE):
            n = h * 3 + d - 1
            block = arecv.at[lax.div(earlier(d), PLANE), :, cols]
            remote(block, block, os.at[n], orr.at[n], {"frame": earlier(d)}).wait_recv()
    for j in range(LINE):
        attn[:, j * width : (j + 1) * width] = arecv[j]

    def project(side, at):
        begin = pl.multiple_of(side * owned + at, 128)
        return jnp.dot(attn[...], wbuf[:, pl.ds(begin, TILE)], preferred_element_type=f32)

    for i in range(owned // TILE):
        at = slice(i * TILE, (i + 1) * TILE)
        pout[:, at] = project(1 - hd, i * TILE).astype(bf)
        send(pout.at[:, at], pin.at[:, at], ps.at[i], pr.at[i], to_pair)
    sum_lanes = jnp.zeros((rows, 128), f32)
    square_lanes = jnp.zeros((rows, 128), f32)
    for i in range(owned // TILE):
        at = slice(i * TILE, (i + 1) * TILE)
        mine = project(hd, i * TILE)
        remote(pout.at[:, at], pin.at[:, at], ps.at[i], pr.at[i], to_pair).wait_recv()
        mine = mine + pin[:, at].astype(f32)
        hidden = (rbuf[:, at].astype(f32) + macc[3, 0:1, at] * mine).astype(bf)
        hidden_ref[:, at] = hidden
        wide = hidden.astype(f32)
        for c in range(0, TILE, 128):
            lane = wide[:, c : c + 128]
            sum_lanes += lane
            square_lanes += lane * lane
    stat[0] = sum_lanes
    stat[1] = square_lanes
    send(stat, stat_in, ss.at[1], sr.at[1], to_pair)
    remote(stat, stat_in, ss.at[1], sr.at[1], to_pair).wait_recv()
    mean = jnp.sum(stat[0] + stat_in[0], axis=1, keepdims=True) / D
    var = jnp.sum(stat[1] + stat_in[1], axis=1, keepdims=True) / D - mean * mean
    row_ref[0] = jnp.broadcast_to(mean, (rows, 128))
    row_ref[1] = jnp.broadcast_to(lax.rsqrt(var + 1e-06), (rows, 128))
    mod_ref[...] = macc[3]
    for copy in sends:
        copy.wait_send()


def finish_kernel(hidden_ref, row_ref, mod_ref, hidden_out, mlp_out):
    hidden = hidden_ref[...]
    hidden_out[...] = hidden
    wide = hidden.astype(jnp.float32)
    mlp_out[...] = (
        (wide - row_ref[0, :, 0:1]) * row_ref[1, :, 0:1] * (1.0 + mod_ref[2:3, :]) + mod_ref[1:2, :]
    ).astype(jnp.bfloat16)


def fused_block(
    residual, query_proj, key_proj, value_proj, q_gain, k_gain, time_embed, time_proj, mod_table, out_weight
):
    rows, cols = query_proj.shape
    width = cols // LINE
    heads_sub = width // HD
    owned = residual.shape[1]
    half_mod = mod_table.shape
    bf, f32 = jnp.bfloat16, jnp.float32
    dma = pltpu.SemaphoreType.DMA
    vmem = pl.BlockSpec(memory_space=pltpu.VMEM)
    hbm = pl.BlockSpec(memory_space=pl.ANY)
    blocks = LINE * PLANE
    count = len(ORDER)
    lines = time_proj.transpose(1, 0, 2)
    out = jax.ShapeDtypeStruct((rows, owned), bf)
    slab = pltpu.VMEM((LINE, rows, width), bf)
    lanes = pltpu.VMEM((2, rows, 128), f32)
    column = pltpu.VMEM((heads_sub, LINE, rows, 1), f32)
    hidden, row, mod = pl.pallas_call(
        block_kernel,
        out_shape=(out, jax.ShapeDtypeStruct((2, rows, 128), f32), jax.ShapeDtypeStruct(half_mod, f32)),
        in_specs=[vmem, vmem, hbm, vmem, vmem, vmem, vmem, hbm, hbm, hbm],
        out_specs=(vmem, vmem, vmem),
        scratch_shapes=[
            pltpu.VMEM((rows, cols), bf),
            pltpu.VMEM((rows, cols), bf),
            pltpu.VMEM((blocks, rows, width), bf),
            pltpu.VMEM((blocks, rows, width), bf),
            slab, slab, slab,
            pltpu.VMEM((rows, cols), bf),
            column, column,
            pltpu.VMEM((heads_sub, LINE, rows, HD), f32),
            lanes, lanes,
            pltpu.VMEM((2,) + half_mod, f32),
            pltpu.VMEM(half_mod, f32),
            pltpu.VMEM((4,) + half_mod, f32),
            pltpu.VMEM((LINE - 1,) + half_mod, f32),
            pltpu.VMEM(half_mod, f32),
            pltpu.VMEM(half_mod, f32),
            pltpu.VMEM(lines.shape, bf),
            pltpu.VMEM(out_weight.shape, bf),
            pltpu.VMEM((rows, owned), bf),
            pltpu.VMEM((rows, owned), bf),
            pltpu.VMEM((rows, owned), bf),
            lanes, lanes,
            dma((3,)), dma((2 + WEIGHT_PARTS,)), dma((9,)), dma((9,)),
        ]
        + [dma((count,))] * 8
        + [dma((3 * heads_sub,))] * 2
        + [dma((6,))] * 2
        + [dma((owned // TILE,))] * 2
        + [dma((2,))] * 2,
        compiler_params=pltpu.CompilerParams(
            collective_id=0, has_side_effects=True, vmem_limit_bytes=60 * 1024 * 1024
        ),
    )(
        query_proj, key_proj, value_proj, q_gain, k_gain,
        time_embed.reshape(1, -1), mod_table, residual, lines, out_weight,
    )
    tile = pl.BlockSpec((rows, TILE), lambda i: (0, i))
    return pl.pallas_call(
        finish_kernel,
        out_shape=(out, out),
        grid=(owned // TILE,),
        in_specs=[
            tile,
            pl.BlockSpec((2, rows, 128), lambda i: (0, 0, 0)),
            pl.BlockSpec((half_mod[0], TILE), lambda i: (0, i)),
        ],
        out_specs=(tile, tile),
        compiler_params=pltpu.CompilerParams(vmem_limit_bytes=60 * 1024 * 1024),
    )(hidden, row, mod)


def accumulate(carry, queries, keys_block, values_block):
    count = keys_block.shape[0]
    heads_here = queries.shape[1]
    keys_three = keys_block.reshape(count, heads_here, HD)
    values_three = values_block.reshape(count, heads_here, HD).astype(jnp.float32)
    scores = jnp.einsum("thd,shd->ths", queries, keys_three, preferred_element_type=jnp.float32) * (
        1.0 / math.sqrt(HD)
    )
    top_old, total_old, summed = carry
    top_new = jnp.maximum(top_old, jnp.max(scores, axis=2))
    weights = jnp.exp(scores - top_new[:, :, None])
    total_new = jnp.sum(weights, axis=2)
    summed_new = jnp.einsum("ths,shd->thd", weights, values_three, precision=lax.Precision.HIGHEST)
    return (top_new, total_new, summed_new)


def shards(
    residual,
    query_proj,
    key_proj,
    value_proj,
    q_gain,
    k_gain,
    time_embed,
    time_proj,
    mod_table,
    out_weight,
):
    if (
        lax.axis_size("head") == 2
        and lax.axis_size("frame") == LINE * PLANE
        and query_proj.shape[1] % (LINE * HD) == 0
    ):
        return fused_block(
            residual, query_proj, key_proj, value_proj, q_gain, k_gain, time_embed, time_proj, mod_table, out_weight
        )
    emb = jax.nn.silu(time_embed)
    partial_mod = jnp.einsum(
        "r,rcd->cd", emb, time_proj.astype(jnp.float32), precision=lax.Precision.HIGHEST
    )
    width = mod_table.shape[1]
    summed_mod = lax.psum(partial_mod, ("frame", "head"))
    share = lax.dynamic_slice_in_dim(summed_mod, lax.axis_index("head") * width, width, 1)
    modulation = mod_table + share
    gate = modulation[0]
    shift = modulation[1]
    scale = modulation[2]
    tok_rows = query_proj.shape[0]
    heads_here = query_proj.shape[1] // HD
    query_wide = query_proj.astype(jnp.float32)
    key_wide = key_proj.astype(jnp.float32)
    total_q, total_k = lax.psum(
        (jnp.sum(query_wide * query_wide, axis=1), jnp.sum(key_wide * key_wide, axis=1)), "head"
    )
    query_rms = lax.rsqrt(total_q / (HEADS * HD) + 1e-06)
    key_rms = lax.rsqrt(total_k / (HEADS * HD) + 1e-06)
    queries = (
        (query_wide * query_rms[:, None] * q_gain)
        .astype(jnp.bfloat16)
        .reshape(tok_rows, heads_here, HD)
    )
    start_state = (
        jnp.full((tok_rows, heads_here), -1e30, jnp.float32),
        jnp.zeros((tok_rows, heads_here), jnp.float32),
        jnp.zeros((tok_rows, heads_here, HD), jnp.float32),
    )
    every_scale = lax.all_gather(key_rms, "frame", axis=0, tiled=True)
    keys_block = (
        lax.all_gather(key_proj, "frame", axis=0, tiled=True).astype(jnp.float32)
        * every_scale[:, None]
        * k_gain
    ).astype(jnp.bfloat16)
    top_final, total_final, summed_final = accumulate(
        start_state, queries, keys_block, lax.all_gather(value_proj, "frame", axis=0, tiled=True)
    )
    attn = (
        (summed_final / total_final[:, :, None])
        .astype(jnp.bfloat16)
        .reshape(tok_rows, heads_here * HD)
    )
    proj = (
        lax.psum_scatter(
            lax.dot_general(
                out_weight, attn, (((0,), (1,)), ((), ())), preferred_element_type=jnp.float32
            ).astype(jnp.bfloat16),
            "head",
            scatter_dimension=0,
            tiled=True,
        )
        .astype(jnp.float32)
        .T
    )
    hidden_out = (residual.astype(jnp.float32) + gate * proj).astype(jnp.bfloat16)
    hidden32 = lax.optimization_barrier(hidden_out).astype(jnp.float32)
    row_sum, row_squares = lax.psum(
        (jnp.sum(hidden32, axis=1), jnp.sum(hidden32 * hidden32, axis=1)), "head"
    )
    mean = row_sum[:, None] / D
    var = row_squares[:, None] / D - mean * mean
    mlp_input = ((hidden32 - mean) * lax.rsqrt(var + 1e-06) * (1.0 + scale) + shift).astype(
        jnp.bfloat16
    )
    return (hidden_out, mlp_input)


def solution(mesh):
    in_specs = (
        P("frame", "head"),
        P("frame", "head"),
        P("frame", "head"),
        P("frame", "head"),
        P("head"),
        P("head"),
        P(("frame", "head")),
        P(("frame", "head"), None, None),
        P(None, "head"),
        P("head", None),
    )
    out_specs = (P("frame", "head"), P("frame", "head"))
    return jax.shard_map(shards, mesh=mesh, in_specs=in_specs, out_specs=out_specs, check_vma=False)
```
